32 devices in a mesh: section: 2 (over y), rows: 4 (over z), heads: 4 (over x, core).
Axes of the slice: x: 2, y: 2, z: 4, core: 2. Of those that a mesh axis runs over, the one named last changes fastest.
Arguments:
- tokens: bfloat16 [2, 2048, 4, 1024], P('section', 'heads', 'rows'), may hold values from -6 to 6
- image_lengths: int32 [2, 4, 6], P(None, 'rows'), may hold values from 64 to 576, as said below
- tile_ranks: int32 [2, 4, 6], P(None, 'rows'), may hold values from 0 to 5, each once within a row
- w_qkv: bfloat16 [1024, 3, 1024], P(None, None, 'heads'), may hold values from -0.1875 to 0.1875
- bias_qv: bfloat16 [2, 1024], P(None, 'heads'), may hold values from -3 to 3
- w_out: bfloat16 [1024, 1024], P('heads'), may hold values from -1.5 to 1.5
- bias_out: bfloat16 [1024], replicated, may hold values from -3 to 3
- w_up: bfloat16 [1024, 4096], P(None, 'heads'), may hold values from -0.1875 to 0.1875
- bias_up: bfloat16 [4096], P('heads'), may hold values from -3 to 3
- w_down: bfloat16 [4096, 1024], P('heads'), may hold values from -0.09375 to 0.09375
- bias_down: bfloat16 [1024], replicated, may hold values from -3 to 3
- ln1_gain: bfloat16 [1024], replicated, may hold values from 0.5 to 1.5
- ln1_bias: bfloat16 [1024], replicated, may hold values from -3 to 3
- ln2_gain: bfloat16 [1024], replicated, may hold values from 0.5 to 1.5
- ln2_bias: bfloat16 [1024], replicated, may hold values from -3 to 3
- grad_out: bfloat16 [2, 2048, 4, 1024], P(None, None, 'rows', ('section', 'heads')), may hold values from -6 to 6
- grad_tap: bfloat16 [2, 2048, 4, 1024], P(None, None, 'rows', ('section', 'heads')), may hold values from -6 to 6
Outputs:
- block_output: bfloat16 [2, 2048, 4, 1024], P(None, None, 'rows', ('section', 'heads'))
- input_tap: bfloat16 [2, 2048, 4, 1024], P(None, None, 'rows', ('section', 'heads'))
- grad_tokens: float32 [2, 2048, 4, 1024], P('section', 'heads', 'rows')
- grad_w_qkv: float32 [1024, 3, 1024], P(None, None, 'heads')
- grad_bias_qv: float32 [2, 1024], P(None, 'heads')
- grad_w_out: float32 [1024, 1024], P('heads')
- grad_bias_out: float32 [1024], replicated
- grad_w_up: float32 [1024, 4096], P(None, 'heads')
- grad_bias_up: float32 [4096], P('heads')
- grad_w_down: float32 [4096, 1024], P('heads')
- grad_bias_down: float32 [1024], replicated
- grad_ln1_gain: float32 [1024], replicated
- grad_ln1_bias: float32 [1024], replicated
- grad_ln2_gain: float32 [1024], replicated
- grad_ln2_bias: float32 [1024], replicated
The draws below stay inside these ranges and needn't reach their ends.
Inputs may be any that keep to these rules, and one draw needn't show every extreme that they name: `image_lengths`: each row holds the patch counts of the 6 images of one sequence, in packing order, summing to 1920; the remaining positions of the 2048 are padding; every row has an image of exactly 576 patches and one of exactly 64. `tile_ranks`: each row is an ordering of the images 0 to 5: their places in the decoder's order.
All inputs are finite; a program needn't handle non-finite values.
Results may differ from the reference program's by a relative error of at most 0.024.
Values may be sent and summed in bfloat16 or wider, within the bound.
A program may use at most 192 MiB of HBM per device.

```python
import jax
import jax.numpy as jnp
from jax import lax

D = 1024
FF = 4096
HD = 64
LEN = 2048
IMGS = 6
SEQS_G = 4
TOTAL = 1920
MOST = 576
MINL = 64
N_SECTION = 2


def draw_image_lengths(key, part):
    row_total = N_SECTION * SEQS_G
    row_keys = jax.random.split(key, row_total)
    spare = TOTAL - IMGS * MINL - (MOST - MINL)

    def one_row(row_key):
        weight_key, order_key = jax.random.split(row_key)
        weights = jax.random.randint(weight_key, (IMGS - 2,), 50, 101).astype(jnp.int32)
        shares = (weights * spare // jnp.sum(weights)).astype(jnp.int32)
        shares = shares.at[0].add(spare - jnp.sum(shares))
        extras = jnp.concatenate([jnp.array([MOST - MINL, 0], jnp.int32), shares])
        placing = jax.random.permutation(order_key, IMGS)
        return jnp.zeros((IMGS,), jnp.int32).at[placing].set(extras) + MINL
    return jax.vmap(one_row)(row_keys).reshape(N_SECTION, SEQS_G, IMGS).astype(jnp.int32)


def block_scale(own_key, shape, cuts, least, top_value):
    factor_of = 1.0
    for dim, parts in cuts:
        heights = jax.random.uniform(jax.random.fold_in(jax.random.fold_in(own_key, 6), dim), (parts,), jnp.float32, least / len(cuts), top_value / len(cuts))
        factor_of = factor_of * jnp.repeat(jnp.exp(heights), shape[dim] // parts).reshape((-1,) + (1,) * (len(shape) - 1 - dim))
    return factor_of


def scatter_about(rng, shape, deviation, most, cuts=(), kind=jnp.bfloat16):
    gain = block_scale(rng, shape, cuts, -0.22, 0.18) if cuts else 1.0
    result = jax.random.normal(rng, shape, jnp.float32) * deviation * gain
    return jnp.minimum(jnp.maximum(result, -most), most).astype(kind)


def setup_inputs(seed: int = 0) -> dict:
    seeds = jax.random.split(jax.random.key(seed), 18)
    return {
        "tokens": scatter_about(seeds[0], (N_SECTION, LEN, SEQS_G, D), 1.0, 6.0, ((0, 2), (1, 4), (2, 4))),
        "image_lengths": draw_image_lengths(jax.random.fold_in(seeds[17], 71), 0),
        "tile_ranks": jax.vmap(lambda own: jax.random.permutation(own, IMGS))(jax.random.split(seeds[2], N_SECTION * SEQS_G)).reshape((N_SECTION, SEQS_G, IMGS)).astype(jnp.int32),
        "w_qkv": scatter_about(seeds[3], (D, 3, D), D ** -0.5, 0.1875, ((2, 4),)),
        "bias_qv": scatter_about(seeds[4], (2, D), 0.3, 3.0, ((1, 4),)),
        "w_out": scatter_about(seeds[5], (D, D), (max(D // 64, 4)) ** -0.5, 1.5, ((0, 4),)),
        "bias_out": scatter_about(seeds[6], (D,), 0.3, 3.0),
        "w_up": scatter_about(seeds[7], (D, FF), D ** -0.5, 0.1875, ((1, 4),)),
        "bias_up": scatter_about(seeds[8], (FF,), 0.3, 3.0, ((0, 4),)),
        "w_down": scatter_about(seeds[9], (FF, D), FF ** -0.5, 0.09375, ((0, 4),)),
        "bias_down": scatter_about(seeds[10], (D,), 0.3, 3.0),
        "ln1_gain": jnp.clip(1.0 + 0.1 * jax.random.normal(seeds[11], (D,), jnp.float32), 0.5, 1.5).astype(jnp.bfloat16),
        "ln1_bias": scatter_about(seeds[12], (D,), 0.3, 3.0),
        "ln2_gain": jnp.clip(1.0 + 0.1 * jax.random.normal(seeds[13], (D,), jnp.float32), 0.5, 1.5).astype(jnp.bfloat16),
        "ln2_bias": scatter_about(seeds[14], (D,), 0.3, 3.0),
        "grad_out": scatter_about(seeds[15], (N_SECTION, LEN, SEQS_G, D), 1.0, 6.0, ((2, 4), (3, 8))),
        "grad_tap": scatter_about(seeds[16], (N_SECTION, LEN, SEQS_G, D), 1.0, 6.0, ((2, 4), (3, 8))),
    }


@jax.custom_vjp
def low(v):
    return lax.optimization_barrier(v.astype(jnp.bfloat16)).astype(jnp.float32)

@jax.custom_vjp
def low_back(v):
    return v

def low_keep(v):
    return (low(v), None)

def low_pass(kept, grad):
    return (grad,)

def back_keep(v):
    return (v, None)

def back_low(kept, grad):
    return (low(grad),)
low.defvjp(low_keep, low_pass)
low_back.defvjp(back_keep, back_low)
EPSILON = 1e-06
MASKED = -1e+30

def exact_dot(left_side, right_side):
    return jnp.dot(left_side, right_side, precision=lax.Precision.HIGHEST)

def layer_norm(values_in, norm_gain, norm_shift):
    average = lax.optimization_barrier(jnp.mean(values_in, axis=-1, keepdims=True))
    centred = values_in - average
    variance = lax.optimization_barrier(jnp.mean(centred * centred, axis=-1, keepdims=True))
    return centred * lax.rsqrt(variance + EPSILON) * norm_gain + norm_shift

def image_tables(lengths, tile_order, extent):
    lengths = lengths.astype(jnp.int32)
    tile_order = tile_order.astype(jnp.int32)
    image_ends = jnp.cumsum(lengths).astype(jnp.int32)
    image_starts = image_ends - lengths
    earlier = (tile_order[None, :] < tile_order[:, None]).astype(jnp.int32)
    new_starts = lax.optimization_barrier(jnp.sum(earlier * lengths[None, :], axis=1)).astype(jnp.int32)
    position = jnp.arange(extent, dtype=jnp.int32)
    segment = lax.optimization_barrier(jnp.sum((position[:, None] >= image_ends[None, :]).astype(jnp.int32), axis=1)).astype(jnp.int32)
    inside_new = (position[:, None] >= new_starts[None, :]) & (position[:, None] < (new_starts + lengths)[None, :])
    source = position + lax.optimization_barrier(jnp.sum(jnp.where(inside_new, image_starts - new_starts, 0), axis=1)).astype(jnp.int32)
    inside_old = segment[:, None] == jnp.arange(lengths.shape[0], dtype=jnp.int32)[None, :]
    target = position + lax.optimization_barrier(jnp.sum(jnp.where(inside_old, new_starts - image_starts, 0), axis=1)).astype(jnp.int32)
    return (segment, source, target)

def attention(query_rows, key_rows, value_rows, segment):
    extent = query_rows.shape[0]
    block_rows = min(512, extent)
    head_total = query_rows.shape[1] // HD
    query_blocks = query_rows.reshape(extent // block_rows, block_rows, head_total, HD)
    key_heads = key_rows.reshape(extent, head_total, HD)
    value_heads = value_rows.reshape(extent, head_total, HD)
    segment_blocks = segment.reshape(extent // block_rows, block_rows)
    score_scale = HD ** (-0.5)

    def one_block(block_item):
        queries, segment_rows = block_item
        raw_scores = jnp.einsum('qhd,khd->hqk', queries, key_heads, precision=lax.Precision.HIGHEST)
        scores = low_back(raw_scores) * score_scale
        allowed = segment_rows[:, None] == segment[None, :]
        scores = jnp.where(allowed[None], scores, MASKED)
        attend_prob = jax.nn.softmax(scores, axis=-1)
        return jnp.einsum('hqk,khd->qhd', low(attend_prob), value_heads, precision=lax.Precision.HIGHEST)
    mixture = lax.map(jax.checkpoint(one_block), (query_blocks, segment_blocks))
    return mixture.reshape(extent, head_total * HD)

def block_forward(row_block, segment, valid_rows, parameters):
    w_qkv, bias_qv, w_out, bias_out, w_up, bias_up, w_down, bias_down, ln1_gain, ln1_bias, ln2_gain, ln2_bias = parameters
    normed_one = low(layer_norm(row_block, ln1_gain, ln1_bias))
    query_rows = low(low_back(exact_dot(normed_one, w_qkv[:, 0]) + bias_qv[0]))
    key_rows = low(low_back(exact_dot(normed_one, w_qkv[:, 1])))
    value_rows = low(low_back(exact_dot(normed_one, w_qkv[:, 2]) + bias_qv[1]))
    attended = low(low_back(attention(query_rows, key_rows, value_rows, segment)))
    attn_sum = low_back(exact_dot(attended, w_out) + bias_out)
    after_attn = row_block + attn_sum
    normed_two = low(layer_norm(after_attn, ln2_gain, ln2_bias))
    pre_act = low_back(exact_dot(normed_two, w_up) + bias_up)
    activated = low(jax.nn.gelu(pre_act, approximate=False))
    mlp_sum = low_back(exact_dot(activated, w_down) + bias_down)
    return (after_attn + mlp_sum) * valid_rows[:, None]

def reference(tokens, image_lengths, tile_ranks, w_qkv, bias_qv, w_out, bias_out, w_up, bias_up, w_down, bias_down, ln1_gain, ln1_bias, ln2_gain, ln2_bias, grad_out, grad_tap):
    seq_total = N_SECTION * SEQS_G

    def seq_major(array_in):
        return jnp.transpose(array_in, (0, 2, 1, 3)).reshape(seq_total, LEN, array_in.shape[-1])

    def back_major(array_in):
        return jnp.transpose(array_in.reshape(N_SECTION, SEQS_G, LEN, array_in.shape[-1]), (0, 2, 1, 3))
    token_rows = seq_major(tokens.astype(jnp.float32))
    grad_rows_dec = seq_major(grad_out.astype(jnp.float32))
    tap_rows_dec = seq_major(grad_tap.astype(jnp.float32))
    length_rows = image_lengths.reshape(seq_total, IMGS)
    order_rows = tile_ranks.reshape(seq_total, IMGS)
    parameters = tuple((weight.astype(jnp.float32) for weight in (w_qkv, bias_qv, w_out, bias_out, w_up, bias_up, w_down, bias_down, ln1_gain, ln1_bias, ln2_gain, ln2_bias)))
    zero_grads = jax.tree.map(jnp.zeros_like, parameters)

    def seq_step(running, seq_item):
        row_block, grad_dec, tap_dec, length_row, order_row = seq_item
        segment, source, target = image_tables(length_row, order_row, LEN)
        valid_rows = (segment < IMGS).astype(jnp.float32)
        block_out, pull_back = jax.vjp(lambda rows_value, param_set: block_forward(rows_value, segment, valid_rows, param_set), row_block, parameters)
        grad_enc = jnp.take(grad_dec, target, axis=0)
        tap_enc = jnp.take(tap_dec, target, axis=0)
        grad_input, grad_params = pull_back(grad_enc)
        running = jax.tree.map(jnp.add, running, grad_params)
        output_dec = jnp.take(block_out, source, axis=0).astype(jnp.bfloat16)
        input_dec = jnp.take(row_block, source, axis=0).astype(jnp.bfloat16)
        return (running, (output_dec, input_dec, grad_input + tap_enc))
    totals, (output_dec, input_dec, grad_input) = lax.scan(seq_step, zero_grads, (token_rows, grad_rows_dec, tap_rows_dec, length_rows, order_rows))
    return (back_major(output_dec), back_major(input_dec), back_major(grad_input), totals[0], totals[1], totals[2], totals[3], totals[4], totals[5], totals[6], totals[7], totals[8], totals[9], totals[10], totals[11])
```

```python
from functools import partial

import jax
import jax.numpy as jnp
from jax import lax
from jax.experimental import pallas as pl
from jax.experimental.pallas import tpu as pltpu
from jax.sharding import PartitionSpec as P

HD = 64
EPSILON = 1e-06
MASKED = -1e30
F32 = jnp.float32
BF = jnp.bfloat16
BQ = 128
BK = 256
LANE = 128
SLOT_XOR = (0, 2, 1, 3)


def nt(a,b): return lax.dot_general(a,b,(((1,),(1,)),((),())),preferred_element_type=F32)
def nn(a,b): return lax.dot_general(a,b,(((1,),(0,)),((),())),preferred_element_type=F32)

def stack_heads(rows, groups, hd):
    lane=lax.broadcasted_iota(jnp.int32, rows.shape, 1)//hd
    zero=jnp.zeros_like(rows)
    return jnp.concatenate([jnp.where(lane==g, rows, zero) for g in range(groups)], axis=0)

def diag_t(acc, groups, hd, bq):
    return jnp.concatenate([acc[g*hd:(g+1)*hd, g*bq:(g+1)*bq] for g in range(groups)], axis=0)

def key_off(slot_ref, kb):
    per=512//BK
    return pl.multiple_of(slot_ref[kb//per]*512 + lax.rem(kb,per)*BK, BK)

def fwd_kernel(groups, hd, lo_ref, hi_ref, slot_ref, q_ref, k_ref, v_ref, sq_ref, sk_ref, o_ref, lse_ref, vt_ref, acc_ref):
    i=pl.program_id(0)
    @pl.when(i==0)
    def _():
        for b in range(v_ref.shape[0]//BK):
            vt_ref[:, b*BK:(b+1)*BK]=jnp.transpose(v_ref[b*BK:(b+1)*BK,:].astype(F32)).astype(BF)
    q4=stack_heads(q_ref[...]*jnp.asarray(hd**-0.5,BF), groups, hd)
    acc_ref[...]=jnp.zeros_like(acc_ref)
    segq=sq_ref[...][0]
    pairs=groups//2
    def step(kb, carry):
        off=key_off(slot_ref,kb)
        kblk=k_ref[pl.ds(off,BK),:]
        mask=sk_ref[pl.ds(off,BK),:]==segq
        mask=jnp.concatenate([mask]*2,axis=1)
        out=[]
        ss=[nt(kblk, q4[g*2*BQ:(g+1)*2*BQ]) for g in range(pairs)]
        for g in range(pairs):
            m,l=carry[g]
            s=jnp.where(mask,ss[g],MASKED)
            m2=jnp.maximum(m,jnp.max(s,axis=0,keepdims=True))
            p=jnp.exp(s-m2)
            a=jnp.exp(m-m2)
            l=l*a+jnp.sum(p,axis=0,keepdims=True)
            pv=nn(vt_ref[g*2*hd:(g+1)*2*hd,pl.ds(off,BK)], p.astype(BF))
            for e in range(2):
                r=slice((2*g+e)*hd,(2*g+e+1)*hd)
                acc_ref[r,:]=acc_ref[r,:]*a[:,e*BQ:(e+1)*BQ]+pv[e*hd:(e+1)*hd,e*BQ:(e+1)*BQ]
            out.append((m2,l))
        return tuple(out)
    init=tuple((jnp.full((1,2*BQ),-jnp.inf,F32),jnp.zeros((1,2*BQ),F32)) for _ in range(pairs))
    res=lax.fori_loop(lo_ref[i],hi_ref[i],step,init)
    m=jnp.concatenate([r[0] for r in res],axis=1)
    l=jnp.concatenate([r[1] for r in res],axis=1)
    inv=1.0/l
    for h in range(groups):
        acc_ref[h*hd:(h+1)*hd,:]*=inv[:,h*BQ:(h+1)*BQ]
    o_ref[...]=jnp.transpose(acc_ref[...]).astype(BF)
    lse_ref[...]=(m+jnp.log(l))[None]

def bwd_kernel(groups, hd, lo_ref, hi_ref, slot_ref, q_ref, k_ref, v_ref, sq_ref, sk_ref, o_ref, lse_ref, do_ref,
               dq_ref, dk_ref, dv_ref, kt_ref, acc_ref, dka_ref, dva_ref):
    i=pl.program_id(0)
    @pl.when(i==0)
    def _():
        for b in range(k_ref.shape[0]//BK):
            kt_ref[:, b*BK:(b+1)*BK]=jnp.transpose(k_ref[b*BK:(b+1)*BK,:].astype(F32)).astype(BF)
        dka_ref[...]=jnp.zeros_like(dka_ref)
        dva_ref[...]=jnp.zeros_like(dva_ref)
    scale=jnp.asarray(hd**-0.5,BF)
    q4=stack_heads(q_ref[...]*scale, groups, hd)
    do=do_ref[...]
    d4=stack_heads(do, groups, hd)
    prod=jnp.transpose(do.astype(F32)*o_ref[...].astype(F32))
    delta=jnp.concatenate([jnp.sum(prod[g*hd:(g+1)*hd],axis=0,keepdims=True) for g in range(groups)],axis=1)
    lse=lse_ref[...][0]
    acc_ref[...]=jnp.zeros_like(acc_ref)
    segq=sq_ref[...][0]
    pairs=groups//2
    w=2*BQ
    def step(kb, carry):
        off=key_off(slot_ref,kb)
        rows=pl.ds(off,BK)
        kblk=k_ref[rows,:]; vblk=v_ref[rows,:]
        mask=sk_ref[rows,:]==segq
        mask=jnp.concatenate([mask]*2,axis=1)
        ss=[(nt(kblk, q4[g*w:(g+1)*w]),nt(vblk, d4[g*w:(g+1)*w])) for g in range(pairs)]
        ps=[];dss=[]
        for g in range(pairs):
            s,dp=ss[g]
            p=jnp.exp(jnp.where(mask,s,MASKED)-lse[:,g*w:(g+1)*w])
            ds=(p*(dp-delta[:,g*w:(g+1)*w])).astype(BF)
            ps.append(p.astype(BF)); dss.append(ds)
            dq=nn(kt_ref[g*2*hd:(g+1)*2*hd,rows], ds)
            for e in range(2):
                r=slice((2*g+e)*hd,(2*g+e+1)*hd)
                acc_ref[r,:]+=dq[e*hd:(e+1)*hd,e*BQ:(e+1)*BQ]
        dva_ref[rows,:]+=nn(jnp.concatenate(ps,axis=1), d4)
        dka_ref[rows,:]+=nn(jnp.concatenate(dss,axis=1), q4)
        return carry
    lax.fori_loop(lo_ref[i],hi_ref[i],step,0)
    dq_ref[...]=(jnp.transpose(acc_ref[...])*(hd**-0.5)).astype(BF)
    @pl.when(i==pl.num_programs(0)-1)
    def _():
        dk_ref[...]=dka_ref[...].astype(BF)
        dv_ref[...]=dva_ref[...].astype(BF)

def _specs(L,W,groups):
    blk=pl.BlockSpec((BQ,W),lambda i,*_:(i,0))
    full=pl.BlockSpec((L,W),lambda i,*_:(0,0))
    sq=pl.BlockSpec((1,1,BQ),lambda i,*_:(i,0,0))
    sk=pl.BlockSpec((L,BQ),lambda i,*_:(0,0))
    st=pl.BlockSpec((1,1,groups*BQ),lambda i,*_:(i,0,0))
    return blk,full,sq,sk,st

def attend_fwd(q,k,v,sq,sk,lo,hi,slot,hd=64):
    L,W=q.shape; groups=W//hd; n=L//BQ
    blk,full,sqs,sks,st=_specs(L,W,groups)
    return pl.pallas_call(partial(fwd_kernel,groups,hd),
      grid_spec=pltpu.PrefetchScalarGridSpec(num_scalar_prefetch=3,grid=(n,),
        in_specs=[blk,full,full,sqs,sks],out_specs=[blk,st],
        scratch_shapes=[pltpu.VMEM((W,L),BF),pltpu.VMEM((W,BQ),F32)]),
      out_shape=[jax.ShapeDtypeStruct((L,W),BF),jax.ShapeDtypeStruct((n,1,groups*BQ),F32)],
      compiler_params=pltpu.CompilerParams(vmem_limit_bytes=32<<20),
      cost_estimate=pl.CostEstimate(flops=8*10**9,transcendentals=5*10**6,bytes_accessed=5<<20),
      name="attend_fwd")(lo,hi,slot,q,k,v,sq,sk)

def attend_bwd(q,k,v,sq,sk,lo,hi,slot,o,lse,do,hd=64):
    L,W=q.shape; groups=W//hd; n=L//BQ
    blk,full,sqs,sks,st=_specs(L,W,groups)
    return pl.pallas_call(partial(bwd_kernel,groups,hd),
      grid_spec=pltpu.PrefetchScalarGridSpec(num_scalar_prefetch=3,grid=(n,),
        in_specs=[blk,full,full,sqs,sks,blk,st,blk],out_specs=[blk,full,full],
        scratch_shapes=[pltpu.VMEM((W,L),BF),pltpu.VMEM((W,BQ),F32),pltpu.VMEM((L,W),F32),pltpu.VMEM((L,W),F32)]),
      out_shape=[jax.ShapeDtypeStruct((L,W),BF)]*3,
      compiler_params=pltpu.CompilerParams(vmem_limit_bytes=40<<20),
      cost_estimate=pl.CostEstimate(flops=20*10**9,transcendentals=5*10**6,bytes_accessed=8<<20),
      name="attend_bwd")(lo,hi,slot,q,k,v,sq,sk,o,lse,do)


def const_spec(shape):
    zeros = (0,) * len(shape)
    return pl.BlockSpec(shape, lambda *_: zeros, pipeline_mode=pl.Buffered(1))


def norm_parts(rows):
    average = jnp.mean(rows, axis=-1, keepdims=True)
    centred = rows - average
    inverse = lax.rsqrt(jnp.mean(centred * centred, axis=-1, keepdims=True) + EPSILON)
    return centred * inverse, inverse


def norm_back(cotangent, normed, inverse):
    first = jnp.mean(cotangent, axis=-1, keepdims=True)
    second = jnp.mean(cotangent * normed, axis=-1, keepdims=True)
    return (cotangent - first - normed * second) * inverse


def column_block(me_ref, e):
    return pl.multiple_of(jnp.bitwise_xor(me_ref[0], e) * LANE, LANE)


def enter_kernel(with_norm, me_ref, t_ref, gain_ref, shift_ref, w_ref, bq_ref, bv_ref, *outs):
    if with_norm:
        h_ref, tap_ref, q_ref, k_ref, v_ref = outs
        normed, _ = norm_parts(t_ref[...].astype(F32))
        h = (normed * gain_ref[...] + shift_ref[...]).astype(BF)
        h_ref[...] = h
        for n, e in enumerate((0, 1, 4, 5)):
            tap_ref[n] = t_ref[:, pl.ds(column_block(me_ref, e), LANE)]
    else:
        q_ref, k_ref, v_ref = outs
        h = t_ref[...]
    q_ref[...] = (nn(h, w_ref[0]) + bq_ref[...]).astype(BF)
    k_ref[...] = nn(h, w_ref[1]).astype(BF)
    v_ref[...] = (nn(h, w_ref[2]) + bv_ref[...]).astype(BF)


def enter(rows, me8, gain, shift, w3, bq, bv, with_norm):
    count, width = rows.shape
    part = w3.shape[2]
    step = min(256, count)
    row = lambda w: pl.BlockSpec((step, w), lambda i, *_: (i, 0))
    outs = [(row(part), jax.ShapeDtypeStruct((count, part), BF))] * 3
    if with_norm:
        outs = [
            (row(width), jax.ShapeDtypeStruct((count, width), BF)),
            (pl.BlockSpec((4, step, LANE), lambda i, *_: (0, i, 0)), jax.ShapeDtypeStruct((4, count, LANE), BF)),
        ] + outs
    return pl.pallas_call(
        partial(enter_kernel, with_norm),
        grid_spec=pltpu.PrefetchScalarGridSpec(
            num_scalar_prefetch=1,
            grid=(count // step,),
            in_specs=[row(width), const_spec((1, width)), const_spec((1, width)), const_spec(w3.shape),
                      const_spec((1, part)), const_spec((1, part))],
            out_specs=[o[0] for o in outs],
        ),
        out_shape=[o[1] for o in outs],
        compiler_params=pltpu.CompilerParams(vmem_limit_bytes=32 << 20),
        cost_estimate=pl.CostEstimate(flops=6 * count * width * part, transcendentals=0, bytes_accessed=6 * count * width),
        name="enter_norm" if with_norm else "enter_plain",
    )(me8, rows, gain, shift, w3, bq, bv)


def reorder_kernel(sources, natural_out, arrays, starts_ref, shifts_ref, out_pos_ref, in_pos_ref, half_ref, *refs):
    ins, outs = refs[: -arrays - 2], refs[-arrays - 2 : -2]
    buf, val = refs[-2:]
    for j in range(2):
        half = jnp.bitwise_xor(half_ref[0], j)
        for a in range(arrays):
            for t, n in enumerate(sources[j][a]):
                rows = ins[n][half] if len(ins[n].shape) == 3 else ins[n][...]
                where_to = pl.ds(pl.multiple_of(in_pos_ref[t] + BQ, BQ), rows.shape[0])
                buf[a, where_to, :] = rows.astype(F32)

        def one_block(i, carry):
            base = out_pos_ref[i]
            place = base + lax.broadcasted_iota(jnp.int32, (BQ, LANE), 0)
            for piece in range(7):
                low = starts_ref[half, piece]
                high = starts_ref[half, piece + 1]

                @pl.when((low < base + BQ) & (high > base))
                def _():
                    keep = (place >= low) & (place < high)
                    for a in range(arrays):
                        rows = buf[a, pl.ds(base + shifts_ref[half, piece] + BQ, BQ), :]
                        val[a] = jnp.where(keep, rows, val[a])

            where_to = pl.ds(pl.multiple_of(i * BQ, BQ), BQ)
            for a in range(arrays):
                outs[a][half if natural_out else j, where_to, :] = val[a].astype(BF)
            return carry

        lax.fori_loop(0, out_pos_ref.shape[0], one_block, 0)


def reorder(operands, sources, natural_out, table, out_pos, in_pos, half, name):
    length = out_pos.shape[0] * BQ
    arrays = len(sources[0])
    return pl.pallas_call(
        partial(reorder_kernel, sources, natural_out, arrays),
        grid_spec=pltpu.PrefetchScalarGridSpec(
            num_scalar_prefetch=5,
            grid=(1,),
            in_specs=[const_spec(o.shape) for o in operands],
            out_specs=[const_spec((2, length, LANE))] * arrays,
            scratch_shapes=[pltpu.VMEM((arrays, length + 2 * BQ, LANE), F32), pltpu.VMEM((arrays, BQ, LANE), F32)],
        ),
        out_shape=[jax.ShapeDtypeStruct((2, length, LANE), BF)] * arrays,
        compiler_params=pltpu.CompilerParams(vmem_limit_bytes=32 << 20),
        cost_estimate=pl.CostEstimate(flops=10**6, transcendentals=0, bytes_accessed=arrays * length * 4 * LANE * 2),
        name=name,
    )(*table, out_pos, in_pos, half, *operands)


TAIL_P = 0.28
TAIL_C = (0.1165205699350068, 0.06749810405563278, 0.2689066993976019, -0.23698906730009697, 0.3898712275439997, -0.10580754284907957)


def erf_tail(x):
    bell = jnp.exp(-0.5 * x * x)
    t = 1.0 / (1.0 + TAIL_P * jnp.abs(x))
    poly = jnp.full_like(t, TAIL_C[-1])
    for c in TAIL_C[-2::-1]:
        poly = poly * t + c
    return poly * t * bell, bell * 0.3989422804014327


def gelu_pair(u):
    tail, density = erf_tail(u)
    cdf = jnp.where(u >= 0.0, 1.0 - tail, tail)
    return u * cdf, cdf + u * density


def assemble(scratch_ref, local_ref, remote_ref, me_ref):
    for n, e in enumerate((0, 1, 4, 5)):
        scratch_ref[e] = local_ref[n]
        scratch_ref[e ^ 2] = remote_ref[n]
    return jnp.concatenate([scratch_ref[jnp.bitwise_xor(me_ref[0], j)] for j in range(8)], axis=1)


def middle_kernel(alias, chunk, me_ref, pos_ref, t_ref, o0, o1, o2, o3, gl_ref, gr_ref, w0, w1, w2, w3, bo_ref, g_ref, b_ref,
                  up0, up1, bu0, bu1, dn0, dn1, bd_ref, *rest):
    rest = rest[alias:]
    x1_ref, h2_ref, gz_ref, a0, a1, d0, d1, dh_ref, zm_ref, zs_ref, db_ref, gs_ref, z_ref = rest
    i = pl.program_id(0)
    attn = nn(o0[...], w0[...]) + nn(o1[...], w1[...]) + nn(o2[...], w2[...]) + nn(o3[...], w3[...])
    x1 = t_ref[...].astype(F32) + (attn + bo_ref[...])
    x1_ref[...] = x1
    normed, _ = norm_parts(x1)
    h2 = (normed * g_ref[...] + b_ref[...]).astype(BF)
    h2_ref[...] = h2
    gz = assemble(gs_ref, gl_ref, gr_ref, me_ref)
    place = pos_ref[i] + lax.broadcasted_iota(jnp.int32, gz.shape, 0)
    gz = jnp.where(place < pos_ref[pos_ref.shape[0] - 1], gz, jnp.zeros_like(gz))
    gz_ref[...] = gz

    @pl.when(i == 0)
    def _():
        db_ref[...] = jnp.zeros_like(db_ref)

    z = x1 + bd_ref[...]
    dh = None
    for half, (up, bu, dn, a, d) in enumerate(((up0, bu0, dn0, a0, d0), (up1, bu1, dn1, a1, d1))):
        for c in range(0, up.shape[1], chunk):
            cols = slice(c, c + chunk)
            u = nn(h2, up[:, cols]) + bu[:, cols]
            back = nt(gz, dn[cols, :])
            act, slope = gelu_pair(u)
            act = act.astype(BF)
            grad = back * slope
            a[:, cols] = act
            du = grad.astype(BF)
            d[:, cols] = du
            db_ref[half : half + 1, cols] += jnp.sum(du.astype(F32), axis=0, keepdims=True)
            if half == 0 and c == 0:
                zp = nn(act, dn[cols, :])
                dh = nt(du, up[:, cols])
            else:
                zp = zp + nn(act, dn[cols, :])
                dh = dh + nt(du, up[:, cols])
    dh_ref[...] = dh.astype(dh_ref.dtype)
    z_ref[0] = z + zp
    z_ref[1] = zp
    for n, e in enumerate((0, 1, 4, 5)):
        zm_ref[n] = z_ref[0, :, pl.ds(column_block(me_ref, e), LANE)]
        zs_ref[n] = z_ref[1, :, pl.ds(column_block(me_ref, e ^ 2), LANE)].astype(BF)


def middle(me8, pos, which, tokens, outs4, g_loc, g_rem, wo4, b_out, gain, shift, ups, bups, downs, b_down, held, dh_type):
    count, width = tokens.shape
    step = min(256, count)
    grid = count // step
    hidden = ups[0].shape[1]
    part = outs4[0].shape[1]
    first = which * grid
    row = lambda w: pl.BlockSpec((step, w), lambda i, *_: (i, 0))
    row_at = lambda w: pl.BlockSpec((step, w), lambda i, *_: (first + i, 0))
    four = pl.BlockSpec((4, step, LANE), lambda i, *_: (0, i, 0))
    four_at = pl.BlockSpec((4, step, LANE), lambda i, *_: (0, first + i, 0))
    in_specs = (
        [row(width)] + [row_at(part)] * 2 + [row(part)] * 2 + [four_at, four]
        + [const_spec((part, width))] * 4 + [const_spec((1, width))] * 3
        + [const_spec((width, hidden))] * 2 + [const_spec((1, hidden))] * 2 + [const_spec((hidden, width))] * 2
        + [const_spec((1, width))]
    )
    operands = [tokens, *outs4, g_loc, g_rem, *wo4, b_out, gain, shift, *ups, *bups, *downs, b_down]
    total = 2 * count
    shared = [(total, width)] * 2 + [(total, hidden)] * 4
    out_shape = (
        [jax.ShapeDtypeStruct((count, width), F32)] + [jax.ShapeDtypeStruct(s, BF) for s in shared]
        + [jax.ShapeDtypeStruct((count, width), dh_type), jax.ShapeDtypeStruct((4, count, LANE), F32),
           jax.ShapeDtypeStruct((4, count, LANE), BF), jax.ShapeDtypeStruct((8, hidden), F32)]
    )
    out_specs = (
        [row(width)] + [row_at(s[1]) for s in shared]
        + [row(width), four, four, pl.BlockSpec((8, hidden), lambda i, *_: (0, 0))]
    )
    aliases = {}
    if held is not None:
        for n, h in enumerate(held):
            aliases[2 + len(operands)] = 1 + n
            operands.append(h)
            in_specs.append(pl.BlockSpec(memory_space=pl.ANY))
    return pl.pallas_call(
        partial(middle_kernel, len(aliases), 512),
        grid_spec=pltpu.PrefetchScalarGridSpec(
            num_scalar_prefetch=2,
            grid=(grid,),
            in_specs=in_specs,
            out_specs=out_specs,
            scratch_shapes=[pltpu.VMEM((8, step, LANE), BF), pltpu.VMEM((2, step, width), F32)],
        ),
        out_shape=out_shape,
        input_output_aliases=aliases,
        compiler_params=pltpu.CompilerParams(vmem_limit_bytes=56 << 20),
        cost_estimate=pl.CostEstimate(flops=18 * count * width * hidden, transcendentals=4 * count * hidden, bytes_accessed=30 << 20),
        name="middle_own" if which == 0 else "middle_partner",
    )(me8, pos, *operands)


def second_kernel(dh_ref, dr_ref, x1_ref, gz_ref, g_ref, w0, w1, w2, w3, dx_ref, ga_ref, do0, do1, dox, sum_ref):
    dh = dh_ref[...] + dr_ref[...].astype(F32)
    normed, inverse = norm_parts(x1_ref[...])
    gz = gz_ref[...].astype(F32)
    dx = norm_back(dh * g_ref[...], normed, inverse) + gz
    dx_ref[...] = dx
    ga = dx.astype(BF)
    ga_ref[...] = ga
    part = w0.shape[0]
    do0[...] = nt(ga, w0[...]).astype(BF)
    do1[...] = nt(ga, w1[...]).astype(BF)
    dox[:, :part] = nt(ga, w2[...]).astype(BF)
    dox[:, part:] = nt(ga, w3[...]).astype(BF)

    @pl.when(pl.program_id(0) == 0)
    def _():
        sum_ref[...] = jnp.zeros_like(sum_ref)

    for n, v in enumerate((dh * normed, dh, ga.astype(F32), gz)):
        sum_ref[n : n + 1, :] += jnp.sum(v, axis=0, keepdims=True)


def second(dh, dr, x1, gz, gain, wo4):
    count, width = dh.shape
    part = wo4[0].shape[0]
    step = min(256, count)
    row = lambda w: pl.BlockSpec((step, w), lambda i: (i, 0))
    return pl.pallas_call(
        second_kernel,
        grid=(count // step,),
        in_specs=[row(width)] * 4 + [const_spec((1, width))] + [const_spec((part, width))] * 4,
        out_specs=[row(width), row(width), row(part), row(part), row(2 * part), pl.BlockSpec((8, width), lambda i: (0, 0))],
        out_shape=[jax.ShapeDtypeStruct((count, width), F32), jax.ShapeDtypeStruct((count, width), BF),
                   jax.ShapeDtypeStruct((count, part), BF), jax.ShapeDtypeStruct((count, part), BF),
                   jax.ShapeDtypeStruct((count, 2 * part), BF), jax.ShapeDtypeStruct((8, width), F32)],
        compiler_params=pltpu.CompilerParams(vmem_limit_bytes=32 << 20),
        cost_estimate=pl.CostEstimate(flops=8 * count * width * part, transcendentals=0, bytes_accessed=14 * count * width),
        name="second_norm_back",
    )(dh, dr, x1, gz, gain, *wo4)


def first_kernel(me_ref, dh_ref, dr_ref, t_ref, dx_ref, gl_ref, gr_ref, g_ref, out_ref, sum_ref, gs_ref):
    dh = dh_ref[...] + dr_ref[...].astype(F32)
    normed, inverse = norm_parts(t_ref[...].astype(F32))
    tap = assemble(gs_ref, gl_ref, gr_ref, me_ref).astype(F32)
    out_ref[...] = norm_back(dh * g_ref[...], normed, inverse) + dx_ref[...] + tap

    @pl.when(pl.program_id(0) == 0)
    def _():
        sum_ref[...] = jnp.zeros_like(sum_ref)

    for n, v in enumerate((dh * normed, dh)):
        sum_ref[n : n + 1, :] += jnp.sum(v, axis=0, keepdims=True)


def first(me8, dh, dr, tokens, dx, tap_loc, tap_rem, gain):
    count, width = dh.shape
    step = min(256, count)
    row = pl.BlockSpec((step, width), lambda i, *_: (i, 0))
    four = pl.BlockSpec((4, step, LANE), lambda i, *_: (0, i, 0))
    return pl.pallas_call(
        first_kernel,
        grid_spec=pltpu.PrefetchScalarGridSpec(
            num_scalar_prefetch=1,
            grid=(count // step,),
            in_specs=[row] * 4 + [four, four, const_spec((1, width))],
            out_specs=[row, pl.BlockSpec((8, width), lambda i, *_: (0, 0))],
            scratch_shapes=[pltpu.VMEM((8, step, LANE), BF)],
        ),
        out_shape=[jax.ShapeDtypeStruct((count, width), F32), jax.ShapeDtypeStruct((8, width), F32)],
        compiler_params=pltpu.CompilerParams(vmem_limit_bytes=32 << 20),
        cost_estimate=pl.CostEstimate(flops=20 * count * width, transcendentals=0, bytes_accessed=16 * count * width),
        name="first_norm_back",
    )(me8, dh, dr, tokens, dx, tap_loc, tap_rem, gain)


def tn(a, b):
    return lax.dot_general(a, b, (((0,), (0,)), ((), ())), preferred_element_type=F32)


def lookup(table, index):
    hit = index[:, None] == jnp.arange(table.shape[0], dtype=jnp.int32)[None, :]
    return jnp.sum(jnp.where(hit, table[None, :], 0), axis=1).astype(jnp.int32)


def running(values):
    count = values.shape[-1]
    upto = jnp.arange(count)[:, None] <= jnp.arange(count)[None, :]
    return jnp.sum(jnp.where(upto, values[..., :, None], 0), axis=-2).astype(jnp.int32)


def order_tables(lengths, ranks, length):
    ends = running(lengths)
    begins = ends - lengths
    earlier = ranks[:, None, :] < ranks[:, :, None]
    moved = jnp.sum(jnp.where(earlier, lengths[:, None, :], 0), axis=2).astype(jnp.int32)
    at_rank = ranks[:, None, :] == jnp.arange(ranks.shape[1], dtype=jnp.int32)[None, :, None]
    by_rank = lambda v: jnp.sum(jnp.where(at_rank, v[:, None, :], 0), axis=2).astype(jnp.int32)
    tail = ends[:, -1:]
    stop = jnp.full_like(tail, length)
    zero = jnp.zeros_like(tail)
    source = (jnp.concatenate([by_rank(moved), tail, stop], axis=1), jnp.concatenate([by_rank(begins - moved), zero], axis=1))
    target = (jnp.concatenate([begins, tail, stop], axis=1), jnp.concatenate([moved - begins, zero], axis=1))
    return ends, source, target


def per_device(tokens, image_lengths, tile_ranks, w_qkv, bias_qv, w_out, bias_out, w_up, bias_up, w_down, bias_down,
               ln1_gain, ln1_bias, ln2_gain, ln2_bias, grad_out, grad_tap):
    own = tokens[0, :, 0, :]
    rows, width = own.shape
    length = 4 * rows
    part = w_out.shape[0]
    section_at = lax.axis_index("section").astype(jnp.int32)
    head_at = lax.axis_index("heads").astype(jnp.int32)
    pair = lambda v: lax.ppermute(v, "heads", [(0, 2), (2, 0), (1, 3), (3, 1)])
    sibling = lambda v: lax.ppermute(v, "heads", [(0, 1), (1, 0), (2, 3), (3, 2)])
    across = lambda v: lax.ppermute(v, "section", [(0, 1), (1, 0)])
    as_row = lambda v: v.astype(F32).reshape(1, -1)
    me8 = (section_at * 4 + head_at).reshape(1)
    half_at = section_at.reshape(1)

    ends_all, source, target = order_tables(image_lengths[:, 0, :], tile_ranks[:, 0, :], length)
    ends = lax.dynamic_index_in_dim(ends_all, section_at, 0, keepdims=False)
    xors = jnp.array(SLOT_XOR, jnp.int32)
    slot_block = jnp.bitwise_xor(head_at, xors)
    slot = lookup(xors, jnp.bitwise_xor(jnp.arange(4, dtype=jnp.int32), head_at))
    slot_pos = slot_block * rows
    row_pos = (slot_pos[:, None] + jnp.arange(rows, dtype=jnp.int32)[None, :]).reshape(-1)
    block_pos = (slot_pos[:, None] + jnp.arange(0, rows, BQ, dtype=jnp.int32)[None, :]).reshape(-1)
    segment = jnp.sum((row_pos[:, None] >= ends[None, :]).astype(jnp.int32), axis=1)
    begins_pad = jnp.concatenate([jnp.zeros((1,), jnp.int32), ends])
    ends_pad = jnp.concatenate([ends, jnp.full((1,), length, jnp.int32)])
    seg_first = jnp.sum((block_pos[:, None] >= ends[None, :]).astype(jnp.int32), axis=1)
    seg_last = jnp.sum((block_pos[:, None] + (BQ - 1) >= ends[None, :]).astype(jnp.int32), axis=1)
    low = lookup(begins_pad, seg_first) // BK
    high = (lookup(ends_pad, seg_last) + BK - 1) // BK
    seg_q = segment.reshape(-1, 1, BQ)
    seg_k = jnp.broadcast_to(segment[:, None], (length, BQ))
    total = ends[-1:]
    valid = (row_pos < total).astype(F32)

    partner = pair(own)
    ups = (w_up, sibling(w_up))
    downs = (w_down, sibling(w_down))
    bups = (as_row(bias_up), as_row(sibling(bias_up)))
    wo_partner = pair(w_out)
    wo4 = (w_out, sibling(w_out), wo_partner, sibling(wo_partner))
    w3 = jnp.transpose(w_qkv, (1, 0, 2))
    w3_sib = sibling(w3)

    back_out, back_tap = reorder([grad_out[:, :, 0, :], grad_tap[:, :, 0, :]], (((0,), (1,)),) * 2, False, target, block_pos,
                                 jnp.zeros((1,), jnp.int32), half_at, "reorder_back")
    both = jnp.stack([back_out[0], back_tap[0], across(back_out[1]), across(back_tap[1])])
    from_sib = sibling(both[:, 2 * rows :])
    g_loc = jnp.stack([both[0, : 2 * rows], from_sib[0], both[2, : 2 * rows], from_sib[2]])
    t_loc = jnp.stack([both[1, : 2 * rows], from_sib[1], both[3, : 2 * rows], from_sib[3]])
    g_rem_own = pair(g_loc[:, rows:])
    g_rem_partner = pair(g_loc[:, :rows])
    t_rem = pair(t_loc[:, rows:])

    gain1, shift1 = as_row(ln1_gain), as_row(ln1_bias)
    bq, bv = as_row(bias_qv[0]), as_row(bias_qv[1])
    h_own, tap_own, q0, k0, v0 = enter(own, me8, gain1, shift1, w3, bq, bv, True)
    h_partner, tap_partner, q1, k1, v1 = enter(partner, me8, gain1, shift1, w3, bq, bv, True)
    h_sib = sibling(h_own)
    h_sib_partner = sibling(h_partner)
    q2, k2, v2 = enter(h_sib, me8, gain1, shift1, w3, bq, bv, False)
    q3, k3, v3 = enter(h_sib_partner, me8, gain1, shift1, w3, bq, bv, False)
    query = jnp.concatenate([q0, q1, q2, q3])
    key = jnp.concatenate([k0, k1, k2, k3])
    value = jnp.concatenate([v0, v1, v2, v3])
    mixed, log_sum = attend_fwd(query, key, value, seg_q, seg_k, low, high, slot)

    def to_decoder(four_own, four_partner):
        keep = jnp.concatenate([four_own, four_partner], axis=1)
        got = sibling(keep[1::2])
        mine = jnp.concatenate([keep[0::2], got], axis=1)
        return mine[0], across(mine[1])

    tap_mine, tap_other = to_decoder(tap_own, tap_partner)

    mixed_sib = sibling(mixed[2 * rows :])
    mixed_loc = jnp.concatenate([mixed[: 2 * rows], mixed_sib], axis=1)
    rem_partner = pair(mixed_loc[:rows])
    rem_own = pair(mixed_loc[rows:])

    gain2, shift2 = as_row(ln2_gain), as_row(ln2_bias)
    b_out, b_down = as_row(bias_out), as_row(bias_down)
    step = min(256, rows)
    pos_of = lambda b: jnp.concatenate([slot_pos[b] + jnp.arange(0, rows, step, dtype=jnp.int32), total])

    def run_middle(which, toks, rem, g_rem, held, dh_type):
        outs4 = (mixed, mixed_sib, rem[:, :part], rem[:, part:])
        return middle(me8, pos_of(which), which, toks, outs4, g_loc, g_rem, wo4, b_out, gain2, shift2,
                      ups, bups, downs, b_down, held, dh_type)

    done1 = run_middle(1, partner, rem_partner, g_rem_partner, None, BF)
    dh_send = done1[7]
    dh_recv = pair(dh_send)
    z_recv1 = pair(done1[9])
    done0 = run_middle(0, own, rem_own, g_rem_own, list(done1[1:7]), F32)
    z_recv0 = pair(done0[9])
    x1_own = done0[0]
    h2, gz, act0, act1, du0, du1 = done0[1:7]
    dh_own = done0[7]
    mask4 = valid[: 2 * rows].reshape(1, 2 * rows, 1)
    y_own = ((done0[8] + z_recv1.astype(F32)) * mask4[:, :rows]).astype(BF)
    y_partner = ((done1[8] + z_recv0.astype(F32)) * mask4[:, rows:]).astype(BF)
    out_mine, out_other = to_decoder(y_own, y_partner)

    natural_blocks = jnp.arange(0, length, BQ, dtype=jnp.int32)

    def slots(v):
        return [v[t * rows : (t + 1) * rows] for t in range(4)]

    four = lambda n: tuple(range(4 * n, 4 * n + 4))
    output_dec, tap_dec = reorder(
        slots(out_mine) + slots(tap_mine) + slots(out_other) + slots(tap_other), ((four(0), four(1)), (four(2), four(3))),
        True, source, natural_blocks, slot_pos, half_at, "reorder_out",
    )

    down_own = tn(act0, gz)
    down_sib = sibling(tn(act1, gz).astype(BF))
    up_own = tn(h2, du0)
    up_sib = sibling(tn(h2, du1).astype(BF))
    grad_down = (down_own + down_sib.astype(F32)).astype(BF)
    grad_up = (up_own + up_sib.astype(F32)).astype(BF)
    grad_down, grad_up = lax.psum((grad_down, grad_up), ("section", "rows"))
    bias_up_part = done0[10][:2] + done1[10][:2]

    dx1, ga, do_own, do_sib, do_x, sums2 = second(dh_own, dh_recv, x1_own, gz[:rows], gain2, wo4)
    do_r = pair(do_x)
    do_for_sib = jnp.concatenate([do_sib, do_r[:, part:]])
    do_from_sib = sibling(do_for_sib)
    grad_mixed = jnp.concatenate([do_own, do_r[:, :part], do_from_sib])
    dq, dk, dv = attend_bwd(query, key, value, seg_q, seg_k, low, high, slot, mixed, log_sum, grad_mixed)

    wo_mine = tn(jnp.concatenate([mixed[:rows], rem_own[:, :part]], axis=1), ga)
    wo_theirs = tn(jnp.concatenate([mixed_sib[:rows], rem_own[:, part:]], axis=1), ga)
    wo_sum = wo_mine + sibling(wo_theirs.astype(BF)).astype(F32)
    grad_wo = wo_sum[:part] + pair(wo_sum[part:].astype(BF)).astype(F32)

    d3 = jnp.stack([dq, dk, dv])
    d3_sib = sibling(d3[:, 2 * rows :])

    def project_back(lo):
        total_back = None
        for n in range(3):
            for piece, weight in ((d3[n, lo : lo + rows], w3[n]), (d3_sib[n, lo : lo + rows], w3_sib[n])):
                term = nt(piece, weight)
                total_back = term if total_back is None else total_back + term
        return total_back

    dh1_recv = pair(project_back(rows).astype(BF))
    dh1_own = project_back(0)
    h_all = jnp.concatenate([h_own, h_partner, h_sib, h_sib_partner])
    grad_w3 = jnp.stack([tn(h_all, dq), tn(h_all, dk), tn(h_all, dv)])
    grad_wo, grad_w3 = lax.psum((grad_wo.astype(BF), grad_w3.astype(BF)), ("section", "rows"))
    grad_tokens, sums1 = first(me8, dh1_own, dh1_recv, own, dx1, t_loc[:, :rows], t_rem, gain1)

    bias_up_own = bias_up_part[0] + sibling(bias_up_part[1])
    bqv = jnp.concatenate([jnp.sum(dq.astype(F32), axis=0), jnp.sum(dv.astype(F32), axis=0)])
    small = lax.psum(jnp.concatenate([sums1[:2], sums2[:4]]), ("section", "rows", "heads"))
    mine = lax.psum(jnp.concatenate([bias_up_own, bqv]), ("section", "rows"))
    hidden = bias_up_own.shape[0]
    return (
        output_dec[:, :, None, :],
        tap_dec[:, :, None, :],
        grad_tokens[None, :, None, :],
        jnp.transpose(grad_w3, (1, 0, 2)).astype(F32),
        mine[hidden:].reshape(2, part),
        grad_wo.astype(F32),
        small[4],
        grad_up.astype(F32),
        mine[:hidden],
        grad_down.astype(F32),
        small[5],
        small[0],
        small[1],
        small[2],
        small[3],
    )


def solution(mesh):
    placed = (
        P("section", "heads", "rows", None),
        P(None, "rows", None),
        P(None, "rows", None),
        P(None, None, "heads"),
        P(None, "heads"),
        P("heads", None),
        P(),
        P(None, "heads"),
        P("heads"),
        P("heads", None),
        P(),
        P(),
        P(),
        P(),
        P(),
        P(None, None, "rows", ("section", "heads")),
        P(None, None, "rows", ("section", "heads")),
    )
    return jax.shard_map(
        per_device,
        mesh=mesh,
        in_specs=placed,
        out_specs=(
            P(None, None, "rows", ("section", "heads")),
            P(None, None, "rows", ("section", "heads")),
            P("section", "heads", "rows", None),
            P(None, None, "heads"),
            P(None, "heads"),
            P("heads", None),
            P(),
            P(None, "heads"),
            P("heads"),
            P("heads", None),
            P(),
            P(),
            P(),
            P(),
            P(),
        ),
        check_vma=False,
    )
```
